512 devices in a mesh: section: 4 (over x), seq: 8 (over y), dp: 16 (over z, core).
Axes of the slice: x: 4, y: 8, z: 8, core: 2. Of those that a mesh axis runs over, the one named last changes fastest.
Arguments:
- queries: bfloat16 [16, 1024, 32, 128], P('dp', 'seq', 'section'), may hold values from -18 to 18
- video_keys: bfloat16 [16, 1024, 32, 128], P('dp', 'seq', 'section'), may hold values from -18 to 18
- video_values: bfloat16 [16, 1024, 32, 128], P('dp', 'seq', 'section'), may hold values from -6 to 6
- cross_queries: bfloat16 [16, 1024, 32, 128], P('dp', 'seq', 'section'), may hold values from -8 to 8
- self_cotangent: bfloat16 [16, 1024, 32, 128], P('dp', 'seq', 'section'), may hold values from -6 to 6
- cross_cotangent: bfloat16 [16, 1024, 32, 128], P('dp', 'seq', 'section'), may hold values from -6 to 6
- caption_states: bfloat16 [16, 512, 4096], P('dp', 'seq'), may hold values from -400 to 400
- caption_gain: float32 [4096], replicated, may hold values from 0.25 to 1.75
- key_weight: bfloat16 [4096, 4096], P('dp', ('section', 'seq')), may hold values from -0.09375 to 0.09375
- value_weight: bfloat16 [4096, 4096], P('dp', ('section', 'seq')), may hold values from -0.09375 to 0.09375
- video_length: int32 [16], replicated, may hold values from 512 to 1024, as said below
- caption_length: int32 [16], replicated, may hold values from 128 to 512, as said below
Outputs:
- query_gradient: bfloat16 [16, 1024, 32, 128], P('dp', 'seq', 'section')
- key_gradient: bfloat16 [16, 1024, 32, 128], P('dp', 'seq', 'section')
- value_gradient: bfloat16 [16, 1024, 32, 128], P('dp', 'seq', 'section')
- cross_query_gradient: bfloat16 [16, 1024, 32, 128], P('dp', 'seq', 'section')
- key_weight_gradient: float32 [4096, 4096], P('dp', ('section', 'seq'))
- value_weight_gradient: float32 [4096, 4096], P('dp', ('section', 'seq'))
The draws below stay inside these ranges and needn't reach their ends.
Inputs may be any that keep to these rules, and one draw needn't show every extreme that they name: `video_length`: some clip has all 1024 tokens valid. `caption_length`: some clip has all 512 caption tokens valid.
All inputs are finite; a program needn't handle non-finite values.
Results may differ from the reference program's by a relative error of at most 0.018.
Values may be sent and summed in bfloat16 or wider, within the bound.
A program may use at most 64 MiB of HBM per device.

```python
import math
import jax
import jax.numpy as jnp
from jax import lax

HEADS = 32
HEAD_SIZE = 128
TEXT_WIDTH = 4096
CAPTION = 512
TOKENS = 1024
CLIPS = 16


def drawn_pair(key):
    shape = (CLIPS, TOKENS, HEADS, HEAD_SIZE)
    base_queries = jnp.clip(jax.random.normal(jax.random.fold_in(key, 101), shape, jnp.float32), -6.0, 6.0)
    base_keys = jnp.clip(jax.random.normal(jax.random.fold_in(key, 102), shape, jnp.float32), -6.0, 6.0)
    return (base_queries, base_keys)


def draw_queries(key, part):
    return drawn_pair(key)[0].astype(jnp.bfloat16)


def draw_video_keys(key, part):
    return drawn_pair(key)[1].astype(jnp.bfloat16)


def draw_caption_states(key, part):
    shape = (CLIPS, CAPTION, TEXT_WIDTH)
    row_scale = jnp.exp(jax.random.uniform(jax.random.fold_in(key, 202), (CLIPS, CAPTION, 1), jnp.float32, 0.0, math.log(10.0)))
    column_scale = jnp.exp(jax.random.uniform(jax.random.fold_in(key, 203), (1, 1, TEXT_WIDTH), jnp.float32, 0.0, math.log(10.0)))
    base = jnp.clip(jax.random.normal(jax.random.fold_in(key, 201), shape, jnp.float32), -4.0, 4.0)
    return (base * row_scale * column_scale).astype(jnp.bfloat16)


def draw_video_length(key, part):
    chosen = jax.random.randint(jax.random.fold_in(key, 301), (), 0, CLIPS)
    values = jax.random.randint(jax.random.fold_in(key, 302), (CLIPS,), TOKENS // 2, TOKENS + 1)
    return jnp.where(jnp.arange(CLIPS) == chosen, TOKENS, values).astype(jnp.int32)


def draw_caption_length(key, part):
    chosen = jax.random.randint(jax.random.fold_in(key, 311), (), 0, CLIPS)
    values = jax.random.randint(jax.random.fold_in(key, 312), (CLIPS,), CAPTION // 4, CAPTION + 1)
    return jnp.where(jnp.arange(CLIPS) == chosen, CAPTION, values).astype(jnp.int32)


def block_scale(stream_key, shape, cuts, smallest, high):
    gain, own = 1.0, jax.random.fold_in(stream_key, 6)
    for dim, parts in cuts:
        heights = jnp.exp(jax.random.uniform(jax.random.fold_in(own, dim), (parts,), jnp.float32, smallest / len(cuts), high / len(cuts)))
        gain = gain * jnp.repeat(heights, shape[dim] // parts).reshape([-1 if axis == dim else 1 for axis in range(len(shape))])
    return gain


def noise(key, dims, spread, bound, cuts=(), kind=jnp.bfloat16):
    entries = spread * jax.random.normal(key, dims, jnp.float32)
    if cuts:
        entries = entries * block_scale(key, dims, cuts, -0.22, 0.18)
    return jnp.clip(entries, -bound, bound).astype(kind)


def setup_inputs(seed: int = 0) -> dict:
    splits = jax.random.split(jax.random.key(seed), 13)
    queries = draw_queries(jax.random.fold_in(splits[12], 71), 0)
    video_keys = draw_video_keys(jax.random.fold_in(splits[12], 71), 0)
    video_values = noise(splits[2], (CLIPS, TOKENS, HEADS, HEAD_SIZE), 1.0, 6.0, ((0, 16), (1, 8), (2, 4)))
    cross_queries = noise(splits[3], (CLIPS, TOKENS, HEADS, HEAD_SIZE), 1.0, 8.0, ((0, 16), (1, 8), (2, 4)))
    self_cotangent = noise(splits[4], (CLIPS, TOKENS, HEADS, HEAD_SIZE), 1.0, 6.0, ((0, 16), (1, 8), (2, 4)))
    cross_cotangent = noise(splits[5], (CLIPS, TOKENS, HEADS, HEAD_SIZE), 1.0, 6.0, ((0, 16), (1, 8), (2, 4)))
    caption_states = draw_caption_states(jax.random.fold_in(splits[12], 71), 0)
    caption_gain = jnp.clip(1.0 + 0.15 * jax.random.normal(splits[7], (TEXT_WIDTH,), jnp.float32), 0.25, 1.75)
    key_weight = noise(splits[8], (TEXT_WIDTH, HEADS * HEAD_SIZE), TEXT_WIDTH ** -0.5, 0.09375, ((0, 16), (1, 32)))
    value_weight = noise(splits[9], (TEXT_WIDTH, HEADS * HEAD_SIZE), TEXT_WIDTH ** -0.5, 0.09375, ((0, 16), (1, 32)))
    video_length = draw_video_length(jax.random.fold_in(splits[12], 71), 0)
    caption_length = draw_caption_length(jax.random.fold_in(splits[12], 71), 0)
    return dict(queries=queries, video_keys=video_keys, video_values=video_values, cross_queries=cross_queries, self_cotangent=self_cotangent, cross_cotangent=cross_cotangent, caption_states=caption_states, caption_gain=caption_gain, key_weight=key_weight, value_weight=value_weight, video_length=video_length, caption_length=caption_length)


norm_epsilon = 1e-06

def normalize_rows(states, caption_gain):
    values = states.astype(jnp.float32)
    mean_square = lax.optimization_barrier(jnp.mean(values * values, axis=-1, keepdims=True))
    return (values * lax.rsqrt(mean_square + norm_epsilon) * caption_gain).astype(jnp.bfloat16)

def head_gradients(query_rows, key_rows, value_rows, cotangent_rows, key_limit):
    score_scale = 1.0 / math.sqrt(HEAD_SIZE)
    scores = jnp.dot(query_rows, key_rows.T, preferred_element_type=jnp.float32) * score_scale
    columns = jnp.arange(key_rows.shape[0], dtype=jnp.int32)[None, :]
    scores = jnp.where(columns < key_limit, scores, -jnp.inf)
    maxima = lax.optimization_barrier(jnp.max(scores, axis=-1, keepdims=True))
    powers = jnp.exp(scores - maxima)
    weights = powers / lax.optimization_barrier(jnp.sum(powers, axis=-1, keepdims=True))
    weights_low = weights.astype(jnp.bfloat16)
    weight_grad = jnp.dot(cotangent_rows, value_rows.T, preferred_element_type=jnp.float32)
    row_total = lax.optimization_barrier(jnp.sum(weights * weight_grad, axis=-1, keepdims=True))
    score_grad = (weights * (weight_grad - row_total) * score_scale).astype(jnp.bfloat16)
    query_grad = jnp.dot(score_grad, key_rows, preferred_element_type=jnp.float32)
    key_grad = jnp.dot(score_grad.T, query_rows, preferred_element_type=jnp.float32)
    value_grad = jnp.dot(weights_low.T, cotangent_rows, preferred_element_type=jnp.float32)
    return (query_grad, key_grad, value_grad)

def all_heads(query_set, key_set, value_set, cotangent_set, key_limit):
    moved = tuple((jnp.moveaxis(tensor, 1, 0) for tensor in (query_set, key_set, value_set, cotangent_set)))

    def per_head(inputs):
        return head_gradients(inputs[0], inputs[1], inputs[2], inputs[3], key_limit)
    results = lax.map(per_head, moved)
    return tuple((jnp.moveaxis(result, 0, 1) for result in results))

def reference(queries, video_keys, video_values, cross_queries, self_cotangent, cross_cotangent, caption_states, caption_gain, key_weight, value_weight, video_length, caption_length):
    head_width = HEADS * HEAD_SIZE
    positions = jnp.arange(TOKENS, dtype=jnp.int32)[:, None, None]

    def one_clip(totals, inputs):
        clip_queries, clip_keys, clip_values, clip_cross, self_rows, cross_rows, states, video_limit, caption_limit = inputs
        normed = normalize_rows(states, caption_gain)
        text_keys = jnp.dot(normed, key_weight, preferred_element_type=jnp.float32).astype(jnp.bfloat16).reshape(CAPTION, HEADS, HEAD_SIZE)
        text_values = jnp.dot(normed, value_weight, preferred_element_type=jnp.float32).astype(jnp.bfloat16).reshape(CAPTION, HEADS, HEAD_SIZE)
        nothing = jnp.zeros((), self_rows.dtype)
        self_rows = jnp.where(positions < video_limit, self_rows, nothing)
        cross_rows = jnp.where(positions < video_limit, cross_rows, nothing)
        query_grad, key_grad, value_grad = all_heads(clip_queries, clip_keys, clip_values, self_rows, video_limit)
        cross_grad, text_key_grad, text_value_grad = all_heads(clip_cross, text_keys, text_values, cross_rows, caption_limit)
        key_cot = text_key_grad.astype(jnp.bfloat16).reshape(CAPTION, head_width)
        value_cot = text_value_grad.astype(jnp.bfloat16).reshape(CAPTION, head_width)
        new_totals = (totals[0] + jnp.dot(normed.T, key_cot, preferred_element_type=jnp.float32), totals[1] + jnp.dot(normed.T, value_cot, preferred_element_type=jnp.float32))
        outputs = (query_grad.astype(jnp.bfloat16), key_grad.astype(jnp.bfloat16), value_grad.astype(jnp.bfloat16), cross_grad.astype(jnp.bfloat16))
        return (new_totals, outputs)
    empty = jnp.zeros((TEXT_WIDTH, head_width), jnp.float32)
    totals, outputs = lax.scan(one_clip, (empty, empty), (queries, video_keys, video_values, cross_queries, self_cotangent, cross_cotangent, caption_states, video_length, caption_length))
    return (outputs[0], outputs[1], outputs[2], outputs[3], totals[0], totals[1])
```

```python
import functools
import math

import jax
import jax.numpy as jnp
from jax import lax
from jax.experimental import pallas as pl
from jax.experimental.pallas import tpu as pltpu
from jax.sharding import PartitionSpec as P

norm_epsilon = 1e-06
f32, bf16 = jnp.float32, jnp.bfloat16
mesh_ids = pl.DeviceIdType.MESH


def far_first(n):
    return sorted(range(1, n), key=lambda k: (-min(k, n - k), k))


def dot(a, b, contract):
    return lax.dot_general(a, b, ((contract[:1], contract[1:]), ((), ())), preferred_element_type=f32)


def kernel(
    sizes,
    blocks, caption, gain, weight, limits,
    video_out, weight_out,
    inbuf, capbuf, normed, wbuf, text, key_turned, key_total, value_total, grads,
    cot_turned, mine, pair_out, pair_in, ring_out, ring_in,
    send, recv, here,
):
    nx, ny, nz = sizes
    tokens, size = inbuf.shape[1:]
    part = tokens // ny
    cap_rows, width = caption.shape
    captions = cap_rows * ny
    quarter = width // nx
    wrows = weight.shape[0]
    s, q, d = lax.axis_index("section"), lax.axis_index("seq"), lax.axis_index("dp")
    z, c = d // 2, lax.rem(d, 2)
    partner = {"dp": 2 * z + 1 - c}
    scale = 1.0 / math.sqrt(size)
    video_limit, caption_limit = limits[0], limits[1]

    def at_x(k):
        return {"section": lax.rem(s + k, nx)}

    def at_y(k):
        return {"seq": lax.rem(q + k, ny)}

    def at_z(k):
        return {"dp": 2 * lax.rem(z + k, nz) + c}

    barrier = pltpu.get_barrier_semaphore()
    peers = [at_x(k) for k in range(1, nx)] + [at_y(k) for k in range(1, ny)]
    peers += [at_z(k) for k in range(1, nz)] + [partner]
    for peer in peers:
        pl.semaphore_signal(barrier, inc=1, device_id=peer, device_id_type=mesh_ids)
    pl.semaphore_wait(barrier, len(peers))

    used = [0]
    every = []

    def push(src, dst, peer):
        n = used[0]
        used[0] += 1
        copy = pltpu.make_async_remote_copy(
            src_ref=src, dst_ref=dst, send_sem=send.at[n], recv_sem=recv.at[n],
            device_id=peer, device_id_type=mesh_ids,
        )
        copy.start()
        every.append(copy)
        return copy

    def rows(index, count):
        return pl.ds(pl.multiple_of(index * count, count), count)

    my_quarter = rows(s, quarter)
    ys, zs = far_first(ny), far_first(nz)

    cap_y = {
        k: push(caption.at[:, my_quarter], capbuf.at[q, :, my_quarter], at_y(k)) for k in ys
    }
    w_z = {k: push(weight, wbuf.at[rows(d, wrows)], at_z(k)) for k in zs}
    w_pair = [push(weight, wbuf.at[rows(d, wrows)], partner)]
    self_y, cross_y = {}, {}
    for k in ys:
        to = lax.rem(q + k, ny)
        self_y[k] = push(
            blocks.at[to, pl.ds(0, 4)], inbuf.at[pl.ds(0, 4), rows(q, part)], at_y(k)
        )
    for k in ys:
        to = lax.rem(q + k, ny)
        cross_y[k] = push(
            blocks.at[to, pl.ds(4, 2)], inbuf.at[pl.ds(4, 2), rows(q, part)], at_y(k)
        )
    own = [
        pltpu.make_async_copy(blocks.at[q], inbuf.at[:, rows(q, part)], here.at[0]),
        pltpu.make_async_copy(caption, capbuf.at[q], here.at[1]),
        pltpu.make_async_copy(weight, wbuf.at[rows(d, wrows)], here.at[2]),
    ]
    for copy in own:
        copy.start()

    cap_x = []
    for k in reversed(ys):
        cap_y[k].wait_recv()
        piece = capbuf.at[lax.rem(q + ny - k, ny), :, my_quarter]
        for j in far_first(nx):
            cap_x.append(push(piece, piece, at_x(j)))
    for k in reversed(zs):
        w_z[k].wait_recv()
        piece = wbuf.at[rows(2 * lax.rem(z + nz - k, nz) + c, wrows)]
        w_pair.append(push(piece, piece, partner))
    for copy in own:
        copy.wait()

    def attend(key, value, query_ref, cot_ref, limit, keys, query_out):
        block = math.gcd(tokens, 256)
        key_turned[:, :keys] = key[...].astype(f32).T.astype(bf16)
        key_total[pl.ds(0, keys)] = jnp.zeros((keys, size), f32)
        value_total[pl.ds(0, keys)] = jnp.zeros((keys, size), f32)

        def step(i, carry):
            span = rows(i, block)
            query = query_ref[span, :]
            at = lax.broadcasted_iota(jnp.int32, (block, size), 0) + i * block
            cot = jnp.where(at < video_limit, cot_ref[span, :].astype(f32), 0.0).astype(bf16)
            scores = dot(key[...], query, (1, 1)) * (scale * math.log2(math.e))
            key_at = lax.broadcasted_iota(jnp.int32, (keys, block), 0)
            scores = jnp.where(key_at < limit, scores, -jnp.inf)
            powers = jnp.exp2(scores - jnp.max(scores, axis=0, keepdims=True))
            inverse = 1.0 / jnp.sum(powers, axis=0, keepdims=True)
            weights = powers * inverse
            weight_grad = dot(value[...], cot, (1, 1))
            total = jnp.sum(weights * weight_grad, axis=0, keepdims=True)
            score_grad = (weights * (weight_grad - total) * scale).astype(bf16)
            value_total[pl.ds(0, keys)] += dot(weights.astype(bf16), cot, (1, 0))
            key_total[pl.ds(0, keys)] += dot(score_grad, query, (1, 0))
            query_out[span, :] = dot(key_turned[:, :keys], score_grad, (1, 0)).T.astype(bf16)
            return carry

        lax.fori_loop(0, tokens // block, step, 0)

    for k in ys:
        self_y[k].wait_recv()
    attend(inbuf.at[1], inbuf.at[2], inbuf.at[0], inbuf.at[3], video_limit, tokens, grads.at[0])
    grads[1] = key_total[...].astype(bf16)
    grads[2] = value_total[...].astype(bf16)
    back = []
    for k in ys:
        to = lax.rem(q + k, ny)
        back.append(
            push(grads.at[pl.ds(0, 3), rows(to, part)], video_out.at[pl.ds(0, 3), q], at_y(k))
        )

    for copy in cap_x + w_pair:
        copy.wait_recv()

    def normalize(i, carry):
        values = capbuf[i].astype(f32)
        mean = jnp.mean(values * values, axis=-1, keepdims=True)
        normed[rows(i, cap_rows), :] = (
            values * lax.rsqrt(mean + norm_epsilon) * gain[...]
        ).astype(bf16)
        return carry

    lax.fori_loop(0, ny, normalize, 0)
    text_block = math.gcd(captions, 256)

    def project(i, carry):
        span = rows(i, text_block)
        text[span, :] = dot(normed[span, :], wbuf[...], (1, 0)).astype(bf16)
        return carry

    lax.fori_loop(0, captions // text_block, project, 0)

    for k in ys:
        cross_y[k].wait_recv()
    attend(
        text.at[:, pl.ds(0, size)], text.at[:, pl.ds(size, size)], inbuf.at[4], inbuf.at[5],
        caption_limit, captions, grads.at[3],
    )
    for k in ys:
        to = lax.rem(q + k, ny)
        back.append(push(grads.at[3, rows(to, part)], video_out.at[3, q], at_y(k)))
    cot_turned[pl.ds(0, size), :] = key_total[pl.ds(0, captions)].T.astype(bf16)
    cot_turned[pl.ds(size, size), :] = value_total[pl.ds(0, captions)].T.astype(bf16)

    order = zs + [0]
    pair, ring = [], []

    def finish(i):
        pair[i].wait_recv()
        total = mine[i] + pair_in[i].astype(f32)
        if i < nz - 1:
            ring_out[i] = total.astype(bf16)
            ring.append(push(ring_out.at[i], ring_in.at[i], at_z(order[i])))
        else:
            mine[i] = total

    for i, k in enumerate(order):
        to = 2 * lax.rem(z + k, nz)
        theirs = dot(cot_turned[...], normed[:, rows(to + 1 - c, wrows)], (1, 0))
        pair_out[i] = theirs.astype(bf16)
        pair.append(push(pair_out.at[i], pair_in.at[i], partner))
        mine[i] = dot(cot_turned[...], normed[:, rows(to + c, wrows)], (1, 0))
        if i:
            finish(i - 1)
    finish(nz - 1)
    keep = pltpu.make_async_copy(grads.at[:, rows(q, part)], video_out.at[:, q], here.at[3])
    keep.start()
    total = mine[nz - 1]
    for i, copy in enumerate(ring):
        copy.wait_recv()
        total += ring_in[i].astype(f32)
    weight_out[...] = total.T
    keep.wait()
    for copy in back:
        copy.wait_recv()
    for copy in every:
        copy.wait_send()


def local(
    sizes,
    queries, video_keys, video_values, cross_queries, self_cotangent, cross_cotangent,
    caption_states, caption_gain, key_weight, value_weight, video_length, caption_length,
):
    nx, ny, nz = sizes
    part, heads, size = queries.shape[1:]
    tokens = part * ny
    cap_rows, width = caption_states.shape[1:]
    captions = cap_rows * ny
    wrows = key_weight.shape[0]
    blocks = jnp.concatenate(
        (queries, video_keys, video_values, self_cotangent, cross_queries, cross_cotangent)
    ).transpose(2, 0, 1, 3)
    clip = lax.axis_index("dp")
    limits = jnp.stack([
        lax.dynamic_index_in_dim(video_length, clip, 0, keepdims=False),
        lax.dynamic_index_in_dim(caption_length, clip, 0, keepdims=False),
    ])
    weight = jnp.concatenate((key_weight, value_weight), axis=1)
    copies = (ny - 1) * (1 + (nx - 1) + 2 + 2) + (nz - 1) + nz + nz + (nz - 1)
    vmem = pl.BlockSpec(memory_space=pltpu.VMEM)
    video, weights = pl.pallas_call(
        functools.partial(kernel, sizes),
        out_shape=(
            jax.ShapeDtypeStruct((4, ny, part, size), bf16),
            jax.ShapeDtypeStruct((wrows, 2 * size), f32),
        ),
        in_specs=[vmem] * 4 + [pl.BlockSpec(memory_space=pltpu.SMEM)],
        out_specs=(vmem, vmem),
        scratch_shapes=[
            pltpu.VMEM((6, tokens, size), bf16),
            pltpu.VMEM((ny, cap_rows, width), bf16),
            pltpu.VMEM((captions, width), bf16),
            pltpu.VMEM((width, 2 * size), bf16),
            pltpu.VMEM((captions, 2 * size), bf16),
            pltpu.VMEM((size, max(tokens, captions)), bf16),
            pltpu.VMEM((max(tokens, captions), size), f32),
            pltpu.VMEM((max(tokens, captions), size), f32),
            pltpu.VMEM((4, tokens, size), bf16),
            pltpu.VMEM((2 * size, captions), bf16),
            pltpu.VMEM((nz, 2 * size, wrows), f32),
            pltpu.VMEM((nz, 2 * size, wrows), bf16),
            pltpu.VMEM((nz, 2 * size, wrows), bf16),
            pltpu.VMEM((nz - 1, 2 * size, wrows), bf16),
            pltpu.VMEM((nz - 1, 2 * size, wrows), bf16),
            pltpu.SemaphoreType.DMA((copies,)),
            pltpu.SemaphoreType.DMA((copies,)),
            pltpu.SemaphoreType.DMA((4,)),
        ],
        compiler_params=pltpu.CompilerParams(
            collective_id=0, has_side_effects=True, vmem_limit_bytes=60 * 1024 * 1024
        ),
    )(blocks, caption_states[0], caption_gain[None], weight, limits)
    video = video.transpose(0, 2, 1, 3)
    return (
        video[0:1], video[1:2], video[2:3], video[3:4],
        weights[:, :size], weights[:, size:],
    )


def solution(mesh):
    token = P("dp", "seq", "section", None)
    weight = P("dp", ("section", "seq"))
    sizes = (mesh.shape["section"], mesh.shape["seq"], mesh.shape["dp"] // 2)
    return jax.shard_map(
        functools.partial(local, sizes),
        mesh=mesh,
        in_specs=(token,) * 6 + (P("dp", "seq", None), P(), weight, weight, P(), P()),
        out_specs=(token,) * 4 + (weight, weight),
        check_vma=False,
    )
```

```python
import functools
import math

import jax
import jax.numpy as jnp
from jax import lax
from jax.experimental import pallas as pl
from jax.experimental.pallas import tpu as pltpu
from jax.sharding import PartitionSpec as P

norm_epsilon = 1e-06
f32, bf16 = jnp.float32, jnp.bfloat16
mesh_ids = pl.DeviceIdType.MESH


def far_first(n):
    return sorted(range(1, n), key=lambda k: (-min(k, n - k), k))


def dot(a, b, contract):
    return lax.dot_general(a, b, ((contract[:1], contract[1:]), ((), ())), preferred_element_type=f32)


def kernel(
    sizes,
    blocks, caption, gain, key_weight, value_weight, video_length, caption_length,
    query_out, key_out, value_out, cross_out, key_weight_out, value_weight_out,
    inbuf, capbuf, normed, wbuf, text, key_turned, key_total, value_total, grads,
    cot_turned, mine, pair_out, pair_in, ring_out, ring_in,
    send, recv, here,
):
    nx, ny, nz = sizes
    tokens, size = inbuf.shape[1:]
    part = tokens // ny
    cap_rows, width = caption.shape
    captions = cap_rows * ny
    quarter = width // nx
    wrows = key_weight.shape[0]
    s, q, d = lax.axis_index("section"), lax.axis_index("seq"), lax.axis_index("dp")
    z, c = d // 2, lax.rem(d, 2)
    partner = {"dp": 2 * z + 1 - c}
    scale = 1.0 / math.sqrt(size)
    video_limit, caption_limit = video_length[d], caption_length[d]

    def at_x(k):
        return {"section": lax.rem(s + k, nx)}

    def at_y(k):
        return {"seq": lax.rem(q + k, ny)}

    def at_z(k):
        return {"dp": 2 * lax.rem(z + k, nz) + c}

    barrier = pltpu.get_barrier_semaphore()
    peers = [at_x(k) for k in range(1, nx)] + [at_y(k) for k in range(1, ny)]
    peers += [at_z(k) for k in range(1, nz)] + [partner]
    for peer in peers:
        pl.semaphore_signal(barrier, inc=1, device_id=peer, device_id_type=mesh_ids)
    pl.semaphore_wait(barrier, len(peers))

    used = [0]
    every = []

    def push(src, dst, peer):
        n = used[0]
        used[0] += 1
        copy = pltpu.make_async_remote_copy(
            src_ref=src, dst_ref=dst, send_sem=send.at[n], recv_sem=recv.at[n],
            device_id=peer, device_id_type=mesh_ids,
        )
        copy.start()
        every.append(copy)
        return copy

    def rows(index, count):
        return pl.ds(pl.multiple_of(index * count, count), count)

    my_quarter = rows(s, quarter)
    ys, zs = far_first(ny), far_first(nz)

    cap_y = {
        k: push(caption.at[:, my_quarter], capbuf.at[q, :, my_quarter], at_y(k)) for k in ys
    }
    mine_w = wbuf.at[rows(d, wrows)]
    own = [
        pltpu.make_async_copy(key_weight, mine_w.at[:, pl.ds(0, size)], here.at[0]),
        pltpu.make_async_copy(value_weight, mine_w.at[:, pl.ds(size, size)], here.at[1]),
        pltpu.make_async_copy(blocks.at[q], inbuf.at[:, rows(q, part)], here.at[2]),
        pltpu.make_async_copy(caption, capbuf.at[q], here.at[3]),
    ]
    for copy in own:
        copy.start()
    self_y, cross_y = {}, {}
    for k in ys:
        to = lax.rem(q + k, ny)
        cross_y[k] = push(
            blocks.at[to, pl.ds(4, 2)], inbuf.at[pl.ds(4, 2), rows(q, part)], at_y(k)
        )
    for k in ys:
        to = lax.rem(q + k, ny)
        self_y[k] = push(
            blocks.at[to, pl.ds(0, 4)], inbuf.at[pl.ds(0, 4), rows(q, part)], at_y(k)
        )
    own[0].wait()
    own[1].wait()
    w_z = {k: push(mine_w, mine_w, at_z(k)) for k in zs}
    w_pair = [push(mine_w, mine_w, partner)]

    near = {}
    for k in reversed(ys):
        cap_y[k].wait_recv()
        piece = capbuf.at[lax.rem(q + ny - k, ny), :, my_quarter]
        near[k] = [push(piece, piece, at_x(j)) for j in sorted({1, nx - 1})]
    passed = {k: [] for k in ys}
    for k in reversed(ys):
        for copy in near[k]:
            copy.wait_recv()
        if nx == 4:
            half = cap_rows // 2
            for j, at in ((1, 0), (3, half)):
                from_quarter = rows(lax.rem(s + nx - j, nx), quarter)
                piece = capbuf.at[lax.rem(q + ny - k, ny), pl.ds(at, half), from_quarter]
                passed[k].append(push(piece, piece, at_x(j)))
    for k in reversed(zs):
        w_z[k].wait_recv()
        piece = wbuf.at[rows(2 * lax.rem(z + nz - k, nz) + c, wrows)]
        w_pair.append(push(piece, piece, partner))
    own[2].wait()
    own[3].wait()

    def normalize(i):
        values = capbuf[i].astype(f32)
        mean = jnp.mean(values * values, axis=-1, keepdims=True)
        normed[rows(i, cap_rows), :] = (
            values * lax.rsqrt(mean + norm_epsilon) * gain[...]
        ).astype(bf16)

    normalize(q)
    for k in reversed(ys):
        for copy in passed[k]:
            copy.wait_recv()
        normalize(lax.rem(q + ny - k, ny))
    for copy in w_pair:
        copy.wait_recv()
    text_block = math.gcd(captions, 256)

    def project(i, carry):
        span = rows(i, text_block)
        text[span, :] = dot(normed[span, :], wbuf[...], (1, 0)).astype(bf16)
        return carry

    lax.fori_loop(0, captions // text_block, project, 0)

    def attend(key, value, query_ref, cot_ref, limit, keys, query_out):
        block = math.gcd(tokens, 256)
        key_turned[:, :keys] = key[...].astype(f32).T.astype(bf16)
        key_total[pl.ds(0, keys)] = jnp.zeros((keys, size), f32)
        value_total[pl.ds(0, keys)] = jnp.zeros((keys, size), f32)

        def step(i, carry):
            span = rows(i, block)
            query = query_ref[span, :]
            at = lax.broadcasted_iota(jnp.int32, (block, size), 0) + i * block
            cot = jnp.where(at < video_limit, cot_ref[span, :].astype(f32), 0.0).astype(bf16)
            scores = dot(key[...], query, (1, 1)) * (scale * math.log2(math.e))
            key_at = lax.broadcasted_iota(jnp.int32, (keys, block), 0)
            scores = jnp.where(key_at < limit, scores, -jnp.inf)
            powers = jnp.exp2(scores - jnp.max(scores, axis=0, keepdims=True))
            inverse = 1.0 / jnp.sum(powers, axis=0, keepdims=True)
            weights = powers * inverse
            weight_grad = dot(value[...], cot, (1, 1))
            total = jnp.sum(weights * weight_grad, axis=0, keepdims=True)
            score_grad = (weights * (weight_grad - total) * scale).astype(bf16)
            value_total[pl.ds(0, keys)] += dot(weights.astype(bf16), cot, (1, 0))
            key_total[pl.ds(0, keys)] += dot(score_grad, query, (1, 0))
            query_out[span, :] = dot(key_turned[:, :keys], score_grad, (1, 0)).T.astype(bf16)
            return carry

        lax.fori_loop(0, tokens // block, step, 0)

    back, kept = [], []

    def give(i, out):
        for k in ys:
            to = lax.rem(q + k, ny)
            back.append(push(grads.at[i, rows(to, part)], out.at[q], at_y(k)))
        copy = pltpu.make_async_copy(grads.at[i, rows(q, part)], out.at[q], here.at[4 + i])
        copy.start()
        kept.append(copy)

    for k in ys:
        cross_y[k].wait_recv()
    attend(
        text.at[:, pl.ds(0, size)], text.at[:, pl.ds(size, size)], inbuf.at[4], inbuf.at[5],
        caption_limit, captions, grads.at[3],
    )
    give(3, cross_out)
    cot_turned[pl.ds(0, size), :] = key_total[pl.ds(0, captions)].T.astype(bf16)
    cot_turned[pl.ds(size, size), :] = value_total[pl.ds(0, captions)].T.astype(bf16)

    order = zs + [0]
    pair, ring = [], []

    def finish(i):
        pair[i].wait_recv()
        total = mine[i] + pair_in[i].astype(f32)
        if i < nz - 1:
            ring_out[i] = total.astype(bf16)
            ring.append(push(ring_out.at[i], ring_in.at[i], at_z(order[i])))
        else:
            mine[i] = total

    for i, k in enumerate(order):
        to = 2 * lax.rem(z + k, nz)
        theirs = dot(cot_turned[...], normed[:, rows(to + 1 - c, wrows)], (1, 0))
        pair_out[i] = theirs.astype(bf16)
        pair.append(push(pair_out.at[i], pair_in.at[i], partner))
        mine[i] = dot(cot_turned[...], normed[:, rows(to + c, wrows)], (1, 0))
        if i:
            finish(i - 1)
    finish(nz - 1)
    for k in ys:
        self_y[k].wait_recv()
    attend(inbuf.at[1], inbuf.at[2], inbuf.at[0], inbuf.at[3], video_limit, tokens, grads.at[0])
    give(0, query_out)
    grads[1] = key_total[...].astype(bf16)
    give(1, key_out)
    grads[2] = value_total[...].astype(bf16)
    give(2, value_out)
    total = mine[nz - 1]
    for i, copy in enumerate(ring):
        copy.wait_recv()
        total += ring_in[i].astype(f32)
    turned = total.T
    key_weight_out[...] = turned[:, :size]
    value_weight_out[...] = turned[:, size:]
    for copy in kept:
        copy.wait()
    for copy in back:
        copy.wait_recv()
    for copy in every:
        copy.wait_send()


def local(
    sizes,
    queries, video_keys, video_values, cross_queries, self_cotangent, cross_cotangent,
    caption_states, caption_gain, key_weight, value_weight, video_length, caption_length,
):
    nx, ny, nz = sizes
    part, heads, size = queries.shape[1:]
    tokens = part * ny
    cap_rows, width = caption_states.shape[1:]
    captions = cap_rows * ny
    wrows = key_weight.shape[0]
    blocks = jnp.concatenate(
        (queries, video_keys, video_values, self_cotangent, cross_queries, cross_cotangent)
    ).transpose(2, 0, 1, 3)
    copies = (ny - 1) * (1 + 4 + 2 + 4) + (nz - 1) + nz + nz + (nz - 1)
    vmem = pl.BlockSpec(memory_space=pltpu.VMEM)
    smem = pl.BlockSpec(memory_space=pltpu.SMEM)
    *video, key_grad, value_grad = pl.pallas_call(
        functools.partial(kernel, sizes),
        out_shape=(
            (jax.ShapeDtypeStruct((ny, part, size), bf16),) * 4
            + (jax.ShapeDtypeStruct((wrows, size), f32),) * 2
        ),
        in_specs=[vmem] * 5 + [smem] * 2,
        out_specs=(vmem,) * 6,
        scratch_shapes=[
            pltpu.VMEM((6, tokens, size), bf16),
            pltpu.VMEM((ny, cap_rows, width), bf16),
            pltpu.VMEM((captions, width), bf16),
            pltpu.VMEM((width, 2 * size), bf16),
            pltpu.VMEM((captions, 2 * size), bf16),
            pltpu.VMEM((size, max(tokens, captions)), bf16),
            pltpu.VMEM((max(tokens, captions), size), f32),
            pltpu.VMEM((max(tokens, captions), size), f32),
            pltpu.VMEM((4, tokens, size), bf16),
            pltpu.VMEM((2 * size, captions), bf16),
            pltpu.VMEM((nz, 2 * size, wrows), f32),
            pltpu.VMEM((nz, 2 * size, wrows), bf16),
            pltpu.VMEM((nz, 2 * size, wrows), bf16),
            pltpu.VMEM((nz - 1, 2 * size, wrows), bf16),
            pltpu.VMEM((nz - 1, 2 * size, wrows), bf16),
            pltpu.SemaphoreType.DMA((copies,)),
            pltpu.SemaphoreType.DMA((copies,)),
            pltpu.SemaphoreType.DMA((8,)),
        ],
        compiler_params=pltpu.CompilerParams(
            collective_id=0, has_side_effects=True, vmem_limit_bytes=60 * 1024 * 1024
        ),
    )(
        blocks, caption_states[0], caption_gain[None], key_weight, value_weight,
        video_length, caption_length,
    )
    return tuple(a.transpose(1, 0, 2)[None] for a in video) + (key_grad, value_grad)


def solution(mesh):
    token = P("dp", "seq", "section", None)
    weight = P("dp", ("section", "seq"))
    sizes = (mesh.shape["section"], mesh.shape["seq"], mesh.shape["dp"] // 2)
    return jax.shard_map(
        functools.partial(local, sizes),
        mesh=mesh,
        in_specs=(token,) * 6 + (P("dp", "seq", None), P(), weight, weight, P(), P()),
        out_specs=(token,) * 4 + (weight, weight),
        check_vma=False,
    )
```

```python
import functools
import math

import jax
import jax.numpy as jnp
from jax import lax
from jax.experimental import pallas as pl
from jax.experimental.pallas import tpu as pltpu
from jax.sharding import PartitionSpec as P

norm_epsilon = 1e-06
f32, bf16 = jnp.float32, jnp.bfloat16
mesh_ids = pl.DeviceIdType.MESH


def far_first(n):
    return sorted(range(1, n), key=lambda k: (-min(k, n - k), k))


def dot(a, b, contract):
    return lax.dot_general(a, b, ((contract[:1], contract[1:]), ((), ())), preferred_element_type=f32)


def kernel(
    sizes,
    blocks, caption, gain, key_weight, value_weight, video_length, caption_length,
    query_out, key_out, value_out, cross_out, key_weight_out, value_weight_out,
    inbuf, capbuf, normed, wbuf, text, key_turned, key_total, value_total, grads,
    cot_turned, mine, pair_out, pair_in, ring_out, ring_in,
    send, recv, here,
):
    nx, ny, nz = sizes
    tokens, size = inbuf.shape[1:]
    part = tokens // ny
    cap_rows, width = caption.shape
    captions = cap_rows * ny
    direct = width // 4
    quarter = (width - direct) // nx
    wrows = key_weight.shape[0]
    s, q, d = lax.axis_index("section"), lax.axis_index("seq"), lax.axis_index("dp")
    z, c = d // 2, lax.rem(d, 2)
    partner = {"dp": 2 * z + 1 - c}
    scale = 1.0 / math.sqrt(size)
    video_limit, caption_limit = video_length[d], caption_length[d]

    def at_x(k):
        return {"section": lax.rem(s + k, nx)}

    def at_y(k):
        return {"seq": lax.rem(q + k, ny)}

    def at_z(k):
        return {"dp": 2 * lax.rem(z + k, nz) + c}

    barrier = pltpu.get_barrier_semaphore()
    peers = [at_x(k) for k in range(1, nx)] + [at_y(k) for k in range(1, ny)]
    peers += [at_z(k) for k in range(1, nz)] + [partner]
    for peer in peers:
        pl.semaphore_signal(barrier, inc=1, device_id=peer, device_id_type=mesh_ids)
    pl.semaphore_wait(barrier, len(peers))

    used = [0]
    every = []

    def push(src, dst, peer):
        n = used[0]
        used[0] += 1
        copy = pltpu.make_async_remote_copy(
            src_ref=src, dst_ref=dst, send_sem=send.at[n], recv_sem=recv.at[n],
            device_id=peer, device_id_type=mesh_ids,
        )
        copy.start()
        every.append(copy)
        return copy

    def rows(index, count):
        return pl.ds(pl.multiple_of(index * count, count), count)

    def features(index):
        return pl.ds(pl.multiple_of(direct + index * quarter, 128), quarter)

    my_quarter, shared = features(s), pl.ds(0, direct)
    ys, zs = far_first(ny), far_first(nz)

    cap_y = {
        k: push(caption.at[:, my_quarter], capbuf.at[q, :, my_quarter], at_y(k)) for k in ys
    }
    cap_d = {k: push(caption.at[:, shared], capbuf.at[q, :, shared], at_y(k)) for k in ys}
    mine_w = wbuf.at[rows(d, wrows)]
    own = [
        pltpu.make_async_copy(key_weight, mine_w.at[:, pl.ds(0, size)], here.at[0]),
        pltpu.make_async_copy(value_weight, mine_w.at[:, pl.ds(size, size)], here.at[1]),
        pltpu.make_async_copy(blocks.at[q], inbuf.at[:, rows(q, part)], here.at[2]),
        pltpu.make_async_copy(caption, capbuf.at[q], here.at[3]),
    ]
    for copy in own:
        copy.start()
    self_y, cross_y = {}, {}
    for k in ys:
        to = lax.rem(q + k, ny)
        cross_y[k] = push(
            blocks.at[to, pl.ds(4, 2)], inbuf.at[pl.ds(4, 2), rows(q, part)], at_y(k)
        )
    for k in ys:
        to = lax.rem(q + k, ny)
        self_y[k] = push(
            blocks.at[to, pl.ds(0, 4)], inbuf.at[pl.ds(0, 4), rows(q, part)], at_y(k)
        )
    own[0].wait()
    own[1].wait()
    w_z = {k: push(mine_w, mine_w, at_z(k)) for k in zs}
    w_pair = [push(mine_w, mine_w, partner)]

    near = {}
    for k in reversed(ys):
        cap_y[k].wait_recv()
        piece = capbuf.at[lax.rem(q + ny - k, ny), :, my_quarter]
        near[k] = [push(piece, piece, at_x(j)) for j in sorted({1, nx - 1})]
    passed = {k: [] for k in ys}
    for k in reversed(ys):
        for copy in near[k]:
            copy.wait_recv()
        if nx == 4:
            half = cap_rows // 2
            for j, at in ((1, 0), (3, half)):
                from_quarter = features(lax.rem(s + nx - j, nx))
                piece = capbuf.at[lax.rem(q + ny - k, ny), pl.ds(at, half), from_quarter]
                passed[k].append(push(piece, piece, at_x(j)))
    for k in reversed(zs):
        w_z[k].wait_recv()
        piece = wbuf.at[rows(2 * lax.rem(z + nz - k, nz) + c, wrows)]
        w_pair.append(push(piece, piece, partner))
    own[2].wait()
    own[3].wait()

    def normalize(i):
        values = capbuf[i].astype(f32)
        mean = jnp.mean(values * values, axis=-1, keepdims=True)
        normed[rows(i, cap_rows), :] = (
            values * lax.rsqrt(mean + norm_epsilon) * gain[...]
        ).astype(bf16)

    normalize(q)
    for k in reversed(ys):
        for copy in passed[k] + [cap_d[k]]:
            copy.wait_recv()
        normalize(lax.rem(q + ny - k, ny))
    for copy in w_pair:
        copy.wait_recv()
    text_block = math.gcd(captions, 256)

    def project(i, carry):
        span = rows(i, text_block)
        text[span, :] = dot(normed[span, :], wbuf[...], (1, 0)).astype(bf16)
        return carry

    lax.fori_loop(0, captions // text_block, project, 0)

    def attend(key, value, query_ref, cot_ref, limit, keys, query_out):
        block = math.gcd(tokens, 256)
        key_turned[:, :keys] = key[...].astype(f32).T.astype(bf16)
        key_total[pl.ds(0, keys)] = jnp.zeros((keys, size), f32)
        value_total[pl.ds(0, keys)] = jnp.zeros((keys, size), f32)

        def step(i, carry):
            span = rows(i, block)
            query = query_ref[span, :]
            at = lax.broadcasted_iota(jnp.int32, (block, size), 0) + i * block
            cot = jnp.where(at < video_limit, cot_ref[span, :].astype(f32), 0.0).astype(bf16)
            scores = dot(key[...], query, (1, 1)) * (scale * math.log2(math.e))
            key_at = lax.broadcasted_iota(jnp.int32, (keys, block), 0)
            scores = jnp.where(key_at < limit, scores, -jnp.inf)
            powers = jnp.exp2(scores - jnp.max(scores, axis=0, keepdims=True))
            inverse = 1.0 / jnp.sum(powers, axis=0, keepdims=True)
            weights = powers * inverse
            weight_grad = dot(value[...], cot, (1, 1))
            total = jnp.sum(weights * weight_grad, axis=0, keepdims=True)
            score_grad = (weights * (weight_grad - total) * scale).astype(bf16)
            value_total[pl.ds(0, keys)] += dot(weights.astype(bf16), cot, (1, 0))
            key_total[pl.ds(0, keys)] += dot(score_grad, query, (1, 0))
            query_out[span, :] = dot(key_turned[:, :keys], score_grad, (1, 0)).T.astype(bf16)
            return carry

        lax.fori_loop(0, tokens // block, step, 0)

    back, kept = [], []

    def give(i, out):
        for k in ys:
            to = lax.rem(q + k, ny)
            back.append(push(grads.at[i, rows(to, part)], out.at[q], at_y(k)))
        copy = pltpu.make_async_copy(grads.at[i, rows(q, part)], out.at[q], here.at[4 + i])
        copy.start()
        kept.append(copy)

    for k in ys:
        cross_y[k].wait_recv()
    attend(
        text.at[:, pl.ds(0, size)], text.at[:, pl.ds(size, size)], inbuf.at[4], inbuf.at[5],
        caption_limit, captions, grads.at[3],
    )
    give(3, cross_out)
    cot_turned[pl.ds(0, size), :] = key_total[pl.ds(0, captions)].T.astype(bf16)
    cot_turned[pl.ds(size, size), :] = value_total[pl.ds(0, captions)].T.astype(bf16)

    order = zs + [0]
    pair, ring = [], []

    def finish(i):
        pair[i].wait_recv()
        total = mine[i] + pair_in[i].astype(f32)
        if i < nz - 1:
            ring_out[i] = total.astype(bf16)
            ring.append(push(ring_out.at[i], ring_in.at[i], at_z(order[i])))
        else:
            mine[i] = total

    for i, k in enumerate(order):
        to = 2 * lax.rem(z + k, nz)
        theirs = dot(cot_turned[...], normed[:, rows(to + 1 - c, wrows)], (1, 0))
        pair_out[i] = theirs.astype(bf16)
        pair.append(push(pair_out.at[i], pair_in.at[i], partner))
        mine[i] = dot(cot_turned[...], normed[:, rows(to + c, wrows)], (1, 0))
        if i:
            finish(i - 1)
    finish(nz - 1)
    for k in ys:
        self_y[k].wait_recv()
    attend(inbuf.at[1], inbuf.at[2], inbuf.at[0], inbuf.at[3], video_limit, tokens, grads.at[0])
    give(0, query_out)
    grads[1] = key_total[...].astype(bf16)
    give(1, key_out)
    grads[2] = value_total[...].astype(bf16)
    give(2, value_out)
    total = mine[nz - 1]
    for i, copy in enumerate(ring):
        copy.wait_recv()
        total += ring_in[i].astype(f32)
    turned = total.T
    key_weight_out[...] = turned[:, :size]
    value_weight_out[...] = turned[:, size:]
    for copy in kept:
        copy.wait()
    for copy in back:
        copy.wait_recv()
    for copy in every:
        copy.wait_send()


def local(
    sizes,
    queries, video_keys, video_values, cross_queries, self_cotangent, cross_cotangent,
    caption_states, caption_gain, key_weight, value_weight, video_length, caption_length,
):
    nx, ny, nz = sizes
    part, heads, size = queries.shape[1:]
    tokens = part * ny
    cap_rows, width = caption_states.shape[1:]
    captions = cap_rows * ny
    wrows = key_weight.shape[0]
    blocks = jnp.concatenate(
        (queries, video_keys, video_values, self_cotangent, cross_queries, cross_cotangent)
    ).transpose(2, 0, 1, 3)
    copies = (ny - 1) * (1 + 1 + 4 + 2 + 4) + (nz - 1) + nz + nz + (nz - 1)
    vmem = pl.BlockSpec(memory_space=pltpu.VMEM)
    smem = pl.BlockSpec(memory_space=pltpu.SMEM)
    *video, key_grad, value_grad = pl.pallas_call(
        functools.partial(kernel, sizes),
        out_shape=(
            (jax.ShapeDtypeStruct((ny, part, size), bf16),) * 4
            + (jax.ShapeDtypeStruct((wrows, size), f32),) * 2
        ),
        in_specs=[vmem] * 5 + [smem] * 2,
        out_specs=(vmem,) * 6,
        scratch_shapes=[
            pltpu.VMEM((6, tokens, size), bf16),
            pltpu.VMEM((ny, cap_rows, width), bf16),
            pltpu.VMEM((captions, width), bf16),
            pltpu.VMEM((width, 2 * size), bf16),
            pltpu.VMEM((captions, 2 * size), bf16),
            pltpu.VMEM((size, max(tokens, captions)), bf16),
            pltpu.VMEM((max(tokens, captions), size), f32),
            pltpu.VMEM((max(tokens, captions), size), f32),
            pltpu.VMEM((4, tokens, size), bf16),
            pltpu.VMEM((2 * size, captions), bf16),
            pltpu.VMEM((nz, 2 * size, wrows), f32),
            pltpu.VMEM((nz, 2 * size, wrows), bf16),
            pltpu.VMEM((nz, 2 * size, wrows), bf16),
            pltpu.VMEM((nz - 1, 2 * size, wrows), bf16),
            pltpu.VMEM((nz - 1, 2 * size, wrows), bf16),
            pltpu.SemaphoreType.DMA((copies,)),
            pltpu.SemaphoreType.DMA((copies,)),
            pltpu.SemaphoreType.DMA((8,)),
        ],
        compiler_params=pltpu.CompilerParams(
            collective_id=0, has_side_effects=True, vmem_limit_bytes=60 * 1024 * 1024
        ),
    )(
        blocks, caption_states[0], caption_gain[None], key_weight, value_weight,
        video_length, caption_length,
    )
    return tuple(a.transpose(1, 0, 2)[None] for a in video) + (key_grad, value_grad)


def solution(mesh):
    token = P("dp", "seq", "section", None)
    weight = P("dp", ("section", "seq"))
    sizes = (mesh.shape["section"], mesh.shape["seq"], mesh.shape["dp"] // 2)
    return jax.shard_map(
        functools.partial(local, sizes),
        mesh=mesh,
        in_specs=(token,) * 6 + (P("dp", "seq", None), P(), weight, weight, P(), P()),
        out_specs=(token,) * 4 + (weight, weight),
        check_vma=False,
    )
```

```python
import functools
import math

import jax
import jax.numpy as jnp
from jax import lax
from jax.experimental import pallas as pl
from jax.experimental.pallas import tpu as pltpu
from jax.sharding import PartitionSpec as P

norm_epsilon = 1e-06
f32, bf16 = jnp.float32, jnp.bfloat16
mesh_ids = pl.DeviceIdType.MESH


def far_first(n):
    return sorted(range(1, n), key=lambda k: (-min(k, n - k), k))


def dot(a, b, contract):
    return lax.dot_general(a, b, ((contract[:1], contract[1:]), ((), ())), preferred_element_type=f32)


def kernel(
    sizes,
    blocks, caption, gain, key_weight, value_weight, video_length, caption_length,
    query_out, key_out, value_out, cross_out, key_weight_out, value_weight_out,
    inbuf, capbuf, normed, wbuf, text, key_turned, key_total, value_total, grads,
    cot_turned, mine, pair_out, pair_in, ring_out, ring_in,
    send, recv, here,
):
    nx, ny, nz = sizes
    tokens, size = inbuf.shape[1:]
    part = tokens // ny
    cap_rows, width = caption.shape
    captions = cap_rows * ny
    quarter = width // nx
    wrows = key_weight.shape[0]
    s, q, d = lax.axis_index("section"), lax.axis_index("seq"), lax.axis_index("dp")
    z, c = d // 2, lax.rem(d, 2)
    partner = {"dp": 2 * z + 1 - c}
    scale = 1.0 / math.sqrt(size)
    video_limit, caption_limit = video_length[d], caption_length[d]

    def at_x(k):
        return {"section": lax.rem(s + k, nx)}

    def at_y(k):
        return {"seq": lax.rem(q + k, ny)}

    def at_z(k):
        return {"dp": 2 * lax.rem(z + k, nz) + c}

    barrier = pltpu.get_barrier_semaphore()
    peers = [at_x(k) for k in range(1, nx)] + [at_y(k) for k in range(1, ny)]
    peers += [at_z(k) for k in range(1, nz)] + [partner]
    for peer in peers:
        pl.semaphore_signal(barrier, inc=1, device_id=peer, device_id_type=mesh_ids)
    pl.semaphore_wait(barrier, len(peers))

    used = [0]
    every = []

    def push(src, dst, peer):
        n = used[0]
        used[0] += 1
        copy = pltpu.make_async_remote_copy(
            src_ref=src, dst_ref=dst, send_sem=send.at[n], recv_sem=recv.at[n],
            device_id=peer, device_id_type=mesh_ids,
        )
        copy.start()
        every.append(copy)
        return copy

    def rows(index, count):
        return pl.ds(pl.multiple_of(index * count, count), count)

    my_quarter = rows(s, quarter)
    ys, zs = far_first(ny), far_first(nz)

    cap_y = {
        k: push(caption.at[:, my_quarter], capbuf.at[q, :, my_quarter], at_y(k)) for k in ys
    }
    mine_w = wbuf.at[rows(d, wrows)]
    own = [
        pltpu.make_async_copy(key_weight, mine_w.at[:, pl.ds(0, size)], here.at[0]),
        pltpu.make_async_copy(value_weight, mine_w.at[:, pl.ds(size, size)], here.at[1]),
        pltpu.make_async_copy(blocks.at[q], inbuf.at[:, rows(q, part)], here.at[2]),
        pltpu.make_async_copy(caption, capbuf.at[q], here.at[3]),
    ]
    for copy in own:
        copy.start()
    self_y, cross_y = {}, {}
    for k in ys:
        to = lax.rem(q + k, ny)
        self_y[k] = push(
            blocks.at[to, pl.ds(0, 4)], inbuf.at[pl.ds(0, 4), rows(q, part)], at_y(k)
        )
    for k in ys:
        to = lax.rem(q + k, ny)
        cross_y[k] = push(
            blocks.at[to, pl.ds(4, 2)], inbuf.at[pl.ds(4, 2), rows(q, part)], at_y(k)
        )
    own[0].wait()
    own[1].wait()
    w_z = {k: push(mine_w, mine_w, at_z(k)) for k in zs}
    w_pair = [push(mine_w, mine_w, partner)]

    near = {}
    for k in reversed(ys):
        cap_y[k].wait_recv()
        piece = capbuf.at[lax.rem(q + ny - k, ny), :, my_quarter]
        near[k] = [push(piece, piece, at_x(j)) for j in sorted({1, nx - 1})]
    passed = {k: [] for k in ys}
    for k in reversed(ys):
        for copy in near[k]:
            copy.wait_recv()
        if nx == 4:
            half = cap_rows // 2
            for j, at in ((1, 0), (3, half)):
                from_quarter = rows(lax.rem(s + nx - j, nx), quarter)
                piece = capbuf.at[lax.rem(q + ny - k, ny), pl.ds(at, half), from_quarter]
                passed[k].append(push(piece, piece, at_x(j)))
    for k in reversed(zs):
        w_z[k].wait_recv()
        piece = wbuf.at[rows(2 * lax.rem(z + nz - k, nz) + c, wrows)]
        w_pair.append(push(piece, piece, partner))
    own[2].wait()
    own[3].wait()

    def attend(key, value, query_ref, cot_ref, limit, keys, query_out):
        block = math.gcd(tokens, 256)
        key_turned[:, :keys] = key[...].astype(f32).T.astype(bf16)
        key_total[pl.ds(0, keys)] = jnp.zeros((keys, size), f32)
        value_total[pl.ds(0, keys)] = jnp.zeros((keys, size), f32)

        def step(i, carry):
            span = rows(i, block)
            query = query_ref[span, :]
            at = lax.broadcasted_iota(jnp.int32, (block, size), 0) + i * block
            cot = jnp.where(at < video_limit, cot_ref[span, :].astype(f32), 0.0).astype(bf16)
            scores = dot(key[...], query, (1, 1)) * (scale * math.log2(math.e))
            key_at = lax.broadcasted_iota(jnp.int32, (keys, block), 0)
            scores = jnp.where(key_at < limit, scores, -jnp.inf)
            powers = jnp.exp2(scores - jnp.max(scores, axis=0, keepdims=True))
            inverse = 1.0 / jnp.sum(powers, axis=0, keepdims=True)
            weights = powers * inverse
            weight_grad = dot(value[...], cot, (1, 1))
            total = jnp.sum(weights * weight_grad, axis=0, keepdims=True)
            score_grad = (weights * (weight_grad - total) * scale).astype(bf16)
            value_total[pl.ds(0, keys)] += dot(weights.astype(bf16), cot, (1, 0))
            key_total[pl.ds(0, keys)] += dot(score_grad, query, (1, 0))
            query_out[span, :] = dot(key_turned[:, :keys], score_grad, (1, 0)).T.astype(bf16)
            return carry

        lax.fori_loop(0, tokens // block, step, 0)

    back, kept = [], []

    def give(i, out):
        for k in ys:
            to = lax.rem(q + k, ny)
            back.append(push(grads.at[i, rows(to, part)], out.at[q], at_y(k)))
        copy = pltpu.make_async_copy(grads.at[i, rows(q, part)], out.at[q], here.at[4 + i])
        copy.start()
        kept.append(copy)

    for k in ys:
        self_y[k].wait_recv()
    attend(inbuf.at[1], inbuf.at[2], inbuf.at[0], inbuf.at[3], video_limit, tokens, grads.at[0])
    give(0, query_out)
    grads[1] = key_total[...].astype(bf16)
    give(1, key_out)
    grads[2] = value_total[...].astype(bf16)
    give(2, value_out)

    def normalize(i):
        values = capbuf[i].astype(f32)
        mean = jnp.mean(values * values, axis=-1, keepdims=True)
        normed[rows(i, cap_rows), :] = (
            values * lax.rsqrt(mean + norm_epsilon) * gain[...]
        ).astype(bf16)

    normalize(q)
    for k in reversed(ys):
        for copy in passed[k]:
            copy.wait_recv()
        normalize(lax.rem(q + ny - k, ny))
    for copy in w_pair:
        copy.wait_recv()
    text_block = math.gcd(captions, 256)

    def project(i, carry):
        span = rows(i, text_block)
        text[span, :] = dot(normed[span, :], wbuf[...], (1, 0)).astype(bf16)
        return carry

    lax.fori_loop(0, captions // text_block, project, 0)

    for k in ys:
        cross_y[k].wait_recv()
    attend(
        text.at[:, pl.ds(0, size)], text.at[:, pl.ds(size, size)], inbuf.at[4], inbuf.at[5],
        caption_limit, captions, grads.at[3],
    )
    give(3, cross_out)
    cot_turned[pl.ds(0, size), :] = key_total[pl.ds(0, captions)].T.astype(bf16)
    cot_turned[pl.ds(size, size), :] = value_total[pl.ds(0, captions)].T.astype(bf16)

    order = zs + [0]
    pair, ring = [], []

    def finish(i):
        pair[i].wait_recv()
        total = mine[i] + pair_in[i].astype(f32)
        if i < nz - 1:
            ring_out[i] = total.astype(bf16)
            ring.append(push(ring_out.at[i], ring_in.at[i], at_z(order[i])))
        else:
            mine[i] = total

    for i, k in enumerate(order):
        to = 2 * lax.rem(z + k, nz)
        theirs = dot(cot_turned[...], normed[:, rows(to + 1 - c, wrows)], (1, 0))
        pair_out[i] = theirs.astype(bf16)
        pair.append(push(pair_out.at[i], pair_in.at[i], partner))
        mine[i] = dot(cot_turned[...], normed[:, rows(to + c, wrows)], (1, 0))
        if i:
            finish(i - 1)
    finish(nz - 1)
    total = mine[nz - 1]
    for i, copy in enumerate(ring):
        copy.wait_recv()
        total += ring_in[i].astype(f32)
    turned = total.T
    key_weight_out[...] = turned[:, :size]
    value_weight_out[...] = turned[:, size:]
    for copy in kept:
        copy.wait()
    for copy in back:
        copy.wait_recv()
    for copy in every:
        copy.wait_send()


def local(
    sizes,
    queries, video_keys, video_values, cross_queries, self_cotangent, cross_cotangent,
    caption_states, caption_gain, key_weight, value_weight, video_length, caption_length,
):
    nx, ny, nz = sizes
    part, heads, size = queries.shape[1:]
    tokens = part * ny
    cap_rows, width = caption_states.shape[1:]
    captions = cap_rows * ny
    wrows = key_weight.shape[0]
    blocks = jnp.concatenate(
        (queries, video_keys, video_values, self_cotangent, cross_queries, cross_cotangent)
    ).transpose(2, 0, 1, 3)
    copies = (ny - 1) * (1 + 4 + 2 + 4) + (nz - 1) + nz + nz + (nz - 1)
    vmem = pl.BlockSpec(memory_space=pltpu.VMEM)
    smem = pl.BlockSpec(memory_space=pltpu.SMEM)
    *video, key_grad, value_grad = pl.pallas_call(
        functools.partial(kernel, sizes),
        out_shape=(
            (jax.ShapeDtypeStruct((ny, part, size), bf16),) * 4
            + (jax.ShapeDtypeStruct((wrows, size), f32),) * 2
        ),
        in_specs=[vmem] * 5 + [smem] * 2,
        out_specs=(vmem,) * 6,
        scratch_shapes=[
            pltpu.VMEM((6, tokens, size), bf16),
            pltpu.VMEM((ny, cap_rows, width), bf16),
            pltpu.VMEM((captions, width), bf16),
            pltpu.VMEM((width, 2 * size), bf16),
            pltpu.VMEM((captions, 2 * size), bf16),
            pltpu.VMEM((size, max(tokens, captions)), bf16),
            pltpu.VMEM((max(tokens, captions), size), f32),
            pltpu.VMEM((max(tokens, captions), size), f32),
            pltpu.VMEM((4, tokens, size), bf16),
            pltpu.VMEM((2 * size, captions), bf16),
            pltpu.VMEM((nz, 2 * size, wrows), f32),
            pltpu.VMEM((nz, 2 * size, wrows), bf16),
            pltpu.VMEM((nz, 2 * size, wrows), bf16),
            pltpu.VMEM((nz - 1, 2 * size, wrows), bf16),
            pltpu.VMEM((nz - 1, 2 * size, wrows), bf16),
            pltpu.SemaphoreType.DMA((copies,)),
            pltpu.SemaphoreType.DMA((copies,)),
            pltpu.SemaphoreType.DMA((8,)),
        ],
        compiler_params=pltpu.CompilerParams(
            collective_id=0, has_side_effects=True, vmem_limit_bytes=60 * 1024 * 1024
        ),
    )(
        blocks, caption_states[0], caption_gain[None], key_weight, value_weight,
        video_length, caption_length,
    )
    return tuple(a.transpose(1, 0, 2)[None] for a in video) + (key_grad, value_grad)


def solution(mesh):
    token = P("dp", "seq", "section", None)
    weight = P("dp", ("section", "seq"))
    sizes = (mesh.shape["section"], mesh.shape["seq"], mesh.shape["dp"] // 2)
    return jax.shard_map(
        functools.partial(local, sizes),
        mesh=mesh,
        in_specs=(token,) * 6 + (P("dp", "seq", None), P(), weight, weight, P(), P()),
        out_specs=(token,) * 4 + (weight, weight),
        check_vma=False,
    )
```
